256 devices in a mesh: freq: 16 (over z, core), tile: 16 (over y, x).
Axes of the slice: x: 4, y: 4, z: 8, core: 2. Of those that a mesh axis runs over, the one named last changes fastest.
Arguments:
- focal_field: bfloat16 [16, 16384, 2, 256], P('freq', 'tile'), may hold values from -6 to 6
- v_factors: bfloat16 [16, 16, 16384, 128], P('freq', None, 'tile'), may hold values from -0.1875 to 0.1875
- u_factors: bfloat16 [16, 16384, 16, 128], P('freq', 'tile'), may hold values from -0.125 to 0.125
- ranks: int32 [16, 16, 16], P('freq', None, 'tile'), may hold values from 16 to 64, as said below
- tile_mask: int32 [16, 16, 16], P('freq', None, 'tile'), may hold values 0 or 1
- initial_focus: bfloat16 [16, 32, 1024, 256], P('tile', None, 'freq'), may hold values from -6 to 6
- mute_starts: int32 [16, 1024, 256], P('tile', 'freq'), may hold values from 1 to 31
- taper: float32 [16, 1024], P('tile', 'freq'), may hold values from 0.3 to 3
Outputs:
- focusing: bfloat16 [16, 32, 1024, 256], P('tile', None, 'freq')
- correlation: float32 [16, 256, 256], P('freq', 'tile')
The draws below stay inside these ranges and needn't reach their ends.
Inputs may be any that keep to these rules, and one draw needn't show every extreme that they name: `ranks`: in every frequency some tile has rank exactly 64; no rank is below 16.
All inputs are finite; a program needn't handle non-finite values. No bound on the sum of `tile_mask` on one device may be relied on, other than what follows from the above.
Results may differ from the reference program's by a relative error of at most 0.009.
Values may be sent and summed in bfloat16 or wider, within the bound.
No kernel may reach another device: no remote copies, remote signals or barrier semaphores. Data moves between devices by JAX's collectives and lax.ppermute only.
A program may use at most 64 MiB of HBM per device.

```python
import math
import jax
import jax.numpy as jnp
from jax import lax

TILE_N = 1024
RANK_MAX = 64
FOCAL = 256
FREQ = 16
TILES = 16
ORDER = 16384
TRACE_LENGTH = 32
SUB = 64
N_FREQ = 16
N_TILE = 16


def draw_ranks(key, part):
    drawn = jax.random.randint(key, (FREQ, TILES, TILES), RANK_MAX // 4, RANK_MAX + 1)
    position = jax.random.randint(jax.random.fold_in(key, 7), (FREQ, 1, 1), 0, TILES * TILES)
    cells = jnp.arange(TILES * TILES, dtype=jnp.int32).reshape(1, TILES, TILES)
    return jnp.where(cells == position, RANK_MAX, drawn).astype(jnp.int32)


def with_ends(result, stream_key, smallest, largest):
    shape = result.shape
    index_at = [jax.random.randint(jax.random.fold_in(stream_key, axis), (), 0, shape[axis]) for axis in range(len(shape))]
    result = result.at[tuple(index_at)].set(smallest)
    longest = shape.index(max(shape))
    index_at[longest] = (index_at[longest] + 1) % shape[longest]
    return result.at[tuple(index_at)].set(largest)


def level_of(key, extent, split, low, high):
    def one(dim, shards_of):
        steps = jax.random.uniform(jax.random.fold_in(jax.random.fold_in(key, 6), dim), (shards_of,), jnp.float32, low / len(split), high / len(split))
        return jnp.repeat(jnp.exp(steps), extent[dim] // shards_of).reshape((-1,) + (1,) * (len(extent) - dim - 1))

    level = one(*split[0])
    for cut in split[1:]:
        level = level * one(*cut)
    return level


def scatter_about(own_key, shape, scale, reach, split=(), kind=jnp.bfloat16):
    result = jax.random.normal(own_key, shape, jnp.float32) * scale
    if len(split) > 0:
        result = level_of(own_key, shape, split, -0.22, 0.18) * result
    return jnp.clip(result, min=-reach, max=reach).astype(kind)


def setup_inputs(seed: int = 0) -> dict:
    splits = jax.random.split(jax.random.key(seed), 9)
    focal_field = scatter_about(splits[0], (FREQ, ORDER, 2, FOCAL), 1.0, 6.0, ((0, 16), (1, 16)))
    v_factors = scatter_about(splits[1], (FREQ, TILES, ORDER, 2 * RANK_MAX), TILE_N ** -0.5, 0.1875, ((0, 16), (2, 16)))
    u_factors = scatter_about(splits[2], (FREQ, ORDER, TILES, 2 * RANK_MAX), (2 * N_TILE * RANK_MAX) ** -0.5, 0.125, ((0, 16), (1, 16)))
    ranks = draw_ranks(jax.random.fold_in(splits[8], 71), 0)
    tile_mask = with_ends((jax.random.randint(splits[4], (FREQ, TILES, TILES), 0, 4) < 3).astype(jnp.int32), jax.random.fold_in(splits[4], 1), 0, 1)
    initial_focus = scatter_about(splits[5], (TILES, TRACE_LENGTH, TILE_N, FOCAL), 1.0, 6.0, ((0, 16), (2, 16)))
    mute_starts = with_ends(jax.random.randint(splits[6], (TILES, TILE_N, FOCAL), 1, TRACE_LENGTH), jax.random.fold_in(splits[6], 1), 1, TRACE_LENGTH - 1).astype(jnp.int32)
    taper = jnp.clip(jnp.exp(math.log(3.0) - 2.3025851 * jax.random.uniform(splits[7], (TILES, TILE_N), jnp.float32) ** level_of(splits[7], (TILES, TILE_N), ((0, 16), (1, 16)), -0.2, 0.2)), 0.3, 3.0)
    return {"focal_field": focal_field, "v_factors": v_factors, "u_factors": u_factors, "ranks": ranks, "tile_mask": tile_mask, "initial_focus": initial_focus, "mute_starts": mute_starts, "taper": taper}


def dft_table(trace_length, freq_count):
    clock_moments = jnp.arange(trace_length, dtype=jnp.float32)
    angular_rate = jnp.arange(freq_count, dtype=jnp.float32) + 1.0
    rotation_radians = 2.0 * math.pi / trace_length * clock_moments[:, None] * angular_rate[None, :]
    return jnp.stack([jnp.cos(rotation_radians), -jnp.sin(rotation_radians)], axis=2) / jnp.sqrt(jnp.float32(freq_count))

def one_frequency(packed):
    field, v_mat, u_mat, rank_f, mask_f = packed
    v_blocks = v_mat.astype(jnp.float32).reshape(TILES, TILES, TILE_N, 2 * RANK_MAX)
    f_blocks = field.astype(jnp.float32).reshape(TILES, TILE_N, 2 * FOCAL)
    moments = jnp.einsum('ijrk,jrc->ijkc', v_blocks, f_blocks)
    real_part = moments[:, :, :RANK_MAX, :FOCAL] - moments[:, :, RANK_MAX:, FOCAL:]
    imag_part = moments[:, :, :RANK_MAX, FOCAL:] + moments[:, :, RANK_MAX:, :FOCAL]
    levels = jnp.arange(RANK_MAX, dtype=jnp.int32)
    retained = ((levels[None, None, :] < rank_f[:, :, None]) & (mask_f[:, :, None] > 0)).astype(jnp.float32)
    coeff_real = lax.optimization_barrier((real_part * retained[..., None]).astype(jnp.bfloat16)).astype(jnp.float32)
    coeff_imag = lax.optimization_barrier((imag_part * retained[..., None]).astype(jnp.bfloat16)).astype(jnp.float32)
    upper = jnp.concatenate([coeff_real, -coeff_imag], axis=2)
    lower = jnp.concatenate([coeff_imag, coeff_real], axis=2)
    u_blocks = u_mat.astype(jnp.float32).reshape(TILES, TILE_N, TILES, 2 * RANK_MAX)
    out_real = jnp.einsum('irjk,ijkn->irn', u_blocks, upper)
    out_imag = jnp.einsum('irjk,ijkn->irn', u_blocks, lower)
    return jnp.stack([out_real, out_imag], axis=2).astype(jnp.bfloat16)

def reference(focal_field, v_factors, u_factors, ranks, tile_mask, initial_focus, mute_starts, taper):
    fields = lax.map(one_frequency, (focal_field, v_factors, u_factors, ranks, tile_mask))
    per_tile = jnp.moveaxis(fields, 1, 0)
    table = dft_table(TRACE_LENGTH, FREQ)
    clock_moments = jnp.arange(TRACE_LENGTH, dtype=jnp.int32)

    def one_tile(packed):
        spectra, start_focus, block_mute_start, weight_row = packed
        trace_signal = jnp.einsum('tfc,frcp->trp', table, spectra.astype(jnp.float32), precision=lax.Precision.HIGHEST)
        silenced_wavefield = jnp.where(clock_moments[:, None, None] < block_mute_start[None, :, :], trace_signal, 0.0)
        focusing = (start_focus.astype(jnp.float32) - silenced_wavefield).astype(jnp.bfloat16)
        widened = focusing.astype(jnp.float32)
        weighted = lax.optimization_barrier((widened * weight_row[None, :, None]).astype(jnp.bfloat16)).astype(jnp.float32)
        grouped = widened.reshape(TRACE_LENGTH, N_FREQ, SUB, FOCAL)
        grouped_weighted = weighted.reshape(TRACE_LENGTH, N_FREQ, SUB, FOCAL)
        terms = jnp.einsum('tsrp,tsrq->spq', grouped, grouped_weighted, precision=lax.Precision.HIGHEST)
        return (focusing, terms)
    focusing, terms = lax.map(one_tile, (per_tile, initial_focus, mute_starts, taper))
    correlation = lax.optimization_barrier(jnp.sum(terms, axis=0)) / float(TILES * TRACE_LENGTH * SUB)
    return (focusing, correlation)
```

```python
import math

import jax
import jax.numpy as jnp
from jax import lax
from jax.sharding import PartitionSpec as P


def dft_table(trace_length, freq_count):
    clock_moments = jnp.arange(trace_length, dtype=jnp.float32)
    angular_rate = jnp.arange(freq_count, dtype=jnp.float32) + 1.0
    rotation_radians = 2.0 * math.pi / trace_length * clock_moments[:, None] * angular_rate[None, :]
    return jnp.stack([jnp.cos(rotation_radians), -jnp.sin(rotation_radians)], axis=2) / jnp.sqrt(
        jnp.float32(freq_count)
    )


def stacked_rhs(received):
    sources = received.shape[0]
    columns = received.shape[3]
    real_c = received[:, :, 0, :]
    imag_c = received[:, :, 1, :]
    upper = jnp.concatenate([real_c, -imag_c], axis=1)
    lower = jnp.concatenate([imag_c, real_c], axis=1)
    return jnp.concatenate([upper, lower], axis=2).reshape(sources * upper.shape[1], 2 * columns)


def body(focal_field, v_factors, u_factors, ranks, tile_mask, initial_focus, mute_starts, taper):
    tile_count = lax.axis_size("tile")
    rank_max = v_factors.shape[3] // 2
    focal_count = focal_field.shape[3]
    tile_rows = focal_field.shape[1]
    flat_field = focal_field[0].reshape(tile_rows, 2 * focal_count)
    moments = jnp.einsum(
        "irk,rc->ikc", v_factors[0], flat_field, preferred_element_type=jnp.float32
    )
    real_part = moments[:, :rank_max, :focal_count] - moments[:, rank_max:, focal_count:]
    imag_part = moments[:, :rank_max, focal_count:] + moments[:, rank_max:, :focal_count]
    levels = jnp.arange(rank_max, dtype=jnp.int32)
    retained = (
        (levels[None, :] < ranks[0, :, 0][:, None]) & (tile_mask[0, :, 0][:, None] > 0)
    ).astype(jnp.float32)
    coeffs = jnp.stack(
        [real_part * retained[:, :, None], imag_part * retained[:, :, None]], axis=2
    ).astype(jnp.bfloat16)
    u_rows = u_factors[0]
    received = lax.all_to_all(coeffs, "tile", split_axis=0, concat_axis=0, tiled=True)
    columns = received.shape[3]
    product = jnp.dot(
        u_rows.reshape(tile_rows, -1), stacked_rhs(received), preferred_element_type=jnp.float32
    )
    fields = product.reshape(tile_rows, 2, columns).astype(jnp.bfloat16)
    trace_length = initial_focus.shape[1]
    gathered = lax.all_to_all(fields[None], "freq", split_axis=1, concat_axis=0, tiled=True)
    dft_weights = dft_table(trace_length, gathered.shape[0])
    trace_signal = jnp.einsum(
        "tfc,fscn->tsn", dft_weights, gathered.astype(jnp.float32), precision=lax.Precision.HIGHEST
    )
    group_rows = trace_signal.shape[1]
    clock_moments = jnp.arange(trace_length, dtype=jnp.int32)
    silenced_wavefield = jnp.where(
        clock_moments[:, None, None] < mute_starts[0][None, :, :], trace_signal, 0.0
    )
    focusing = (initial_focus[0].astype(jnp.float32) - silenced_wavefield).astype(jnp.bfloat16)
    weighted = (focusing.astype(jnp.float32) * taper[0][None, :, None]).astype(jnp.bfloat16)
    flat_focus = focusing.reshape(trace_length * group_rows, focal_count)
    flat_weighted = weighted.reshape(trace_length * group_rows, focal_count)
    partial_value = lax.dot_general(
        flat_focus, flat_weighted, (((0,), (0,)), ((), ())), preferred_element_type=jnp.float32
    )
    normalizer = 1.0 / float(tile_count * trace_length * group_rows)
    shares = lax.all_to_all(
        partial_value.astype(jnp.bfloat16), "tile", split_axis=0, concat_axis=0, tiled=True
    )
    share_rows = focal_count // tile_count
    own_rows = jnp.sum(
        shares.reshape(tile_count, share_rows, focal_count).astype(jnp.float32), axis=0
    )
    return (focusing[None], (own_rows * normalizer)[None])


def solution(mesh):
    placed = (
        P("freq", "tile", None, None),
        P("freq", None, "tile", None),
        P("freq", "tile", None, None),
        P("freq", None, "tile"),
        P("freq", None, "tile"),
        P("tile", None, "freq", None),
        P("tile", "freq", None),
        P("tile", "freq"),
    )
    return jax.shard_map(
        body,
        mesh=mesh,
        in_specs=placed,
        out_specs=(P("tile", None, "freq", None), P("freq", "tile", None)),
        check_vma=False,
    )
```

```python
import functools
import math

import jax
import jax.numpy as jnp
from jax import lax
from jax.experimental import pallas as pl
from jax.experimental.pallas import tpu as pltpu
from jax.sharding import PartitionSpec as P


LANES = 128
ORDER = ((1, 7), (2, 6), (3, 5), (4, 0))


def spec(block=None, index=None):
    if block is None:
        return pl.BlockSpec(memory_space=pltpu.VMEM)
    return pl.BlockSpec(block, index)


def moments_kernel(ranks, mask, field_hbm, v_hbm, out, field, v_all, field_t, sems):
    rows, _, focal = field.shape
    tiles, _, wide = v_all.shape
    groups = sems.shape[0] - 1
    group = tiles // groups
    fetch = pltpu.make_async_copy(field_hbm, field, sems.at[groups])
    fetch.start()
    fetches = [
        pltpu.make_async_copy(
            v_hbm.at[pl.ds(s * group, group)], v_all.at[pl.ds(s * group, group)], sems.at[s]
        )
        for s in range(groups)
    ]
    for copy in fetches:
        copy.start()
    source = lax.broadcasted_iota(jnp.int32, (2 * LANES, 2 * LANES), 0)
    target = lax.broadcasted_iota(jnp.int32, (2 * LANES, 2 * LANES), 1)
    wanted = 2 * lax.rem(target, LANES) + lax.div(target, LANES)
    apart = (source == wanted).astype(jnp.float32).astype(jnp.bfloat16)
    lane = lax.broadcasted_iota(jnp.int32, (focal, wide), 1)
    sign = jnp.where(lane < wide // 2, -1.0, 1.0)
    level = lax.rem(lane, wide // 2)
    fetch.wait()
    for b in range(rows // LANES):
        for q in range(focal // LANES):
            block = field[b * LANES : (b + 1) * LANES, :, q * LANES : (q + 1) * LANES]
            turned = lax.dot_general(
                block.reshape(2 * LANES, LANES),
                apart,
                (((0,), (0,)), ((), ())),
                preferred_element_type=jnp.float32,
            ).astype(jnp.bfloat16)
            at = slice(b * LANES, (b + 1) * LANES)
            field_t[q * LANES : (q + 1) * LANES, at] = turned[:, :LANES]
            field_t[focal + q * LANES : focal + (q + 1) * LANES, at] = turned[:, LANES:]
    for s in range(groups):
        fetches[s].wait()
        both = jnp.concatenate([v_all[s * group + n] for n in range(group)], axis=1)
        products = jnp.dot(field_t[...], both, preferred_element_type=jnp.float32)
        for n in range(group):
            i = s * group + n
            a = products[:focal, n * wide : (n + 1) * wide]
            b = products[focal:, n * wide : (n + 1) * wide]
            moments = a + sign * pltpu.roll(b, wide // 2, 1)
            kept = jnp.where(mask[i] > 0, ranks[i], 0)
            out[i] = jnp.where(level < kept, moments, 0.0).astype(jnp.bfloat16)


def moments(ranks, mask, field, v_tiles, groups=2):
    tiles, rows, wide = v_tiles.shape
    focal = field.shape[2]
    return pl.pallas_call(
        moments_kernel,
        in_specs=[
            pl.BlockSpec(memory_space=pltpu.SMEM),
            pl.BlockSpec(memory_space=pltpu.SMEM),
            pl.BlockSpec(memory_space=pltpu.HBM),
            pl.BlockSpec(memory_space=pltpu.HBM),
        ],
        out_specs=spec(),
        scratch_shapes=[
            pltpu.VMEM(field.shape, jnp.bfloat16),
            pltpu.VMEM(v_tiles.shape, jnp.bfloat16),
            pltpu.VMEM((2 * focal, rows), jnp.bfloat16),
            pltpu.SemaphoreType.DMA((groups + 1,)),
        ],
        out_shape=jax.ShapeDtypeStruct((tiles, focal, wide), jnp.bfloat16),
        cost_estimate=pl.CostEstimate(
            flops=4 * tiles * rows * wide * focal, bytes_accessed=6 << 20, transcendentals=0
        ),
        compiler_params=pltpu.CompilerParams(vmem_limit_bytes=60 << 20),
        name="moments",
    )(ranks, mask, field, v_tiles)


def flatten_kernel(place, u_tiles, u_rows):
    rows = u_tiles.shape[0]
    u_rows[...] = u_tiles[...].reshape(rows, -1)


def flatten(place, u_tiles, distances, chips):
    rows, tiles, wide = u_tiles.shape
    block = rows // chips

    def source(s, where):
        ahead = sum((jnp.where(s == n, d, 0) for n, d in enumerate(distances)), 0)
        return (lax.rem(where[0] + ahead, chips), 0, 0)

    return pl.pallas_call(
        flatten_kernel,
        grid_spec=pltpu.PrefetchScalarGridSpec(
            num_scalar_prefetch=1,
            grid=(len(distances),),
            in_specs=[spec((block, tiles, wide), source)],
            out_specs=spec((block, tiles * wide), lambda s, where: (s, 0)),
        ),
        out_shape=jax.ShapeDtypeStruct((len(distances) * block, tiles * wide), jnp.bfloat16),
        cost_estimate=pl.CostEstimate(flops=1 << 22, bytes_accessed=8 << 20, transcendentals=0),
        compiler_params=pltpu.CompilerParams(vmem_limit_bytes=60 << 20),
    )(place, u_tiles)


def terms_kernel(received, terms):
    tiles, focal, wide = received.shape
    lane = lax.broadcasted_iota(jnp.int32, (focal, wide), 1)
    sign = jnp.where(lane < wide // 2, 1.0, -1.0)
    for j in range(tiles):
        coeffs = received[j].astype(jnp.float32)
        at = slice(j * wide, (j + 1) * wide)
        terms[:focal, at] = (coeffs * sign).astype(jnp.bfloat16)
        terms[focal:, at] = pltpu.roll(coeffs, wide // 2, 1).astype(jnp.bfloat16)


def rank_terms(received):
    tiles, focal, wide = received.shape
    return pl.pallas_call(
        terms_kernel,
        in_specs=[spec()],
        out_specs=spec(),
        out_shape=jax.ShapeDtypeStruct((2 * focal, tiles * wide), jnp.bfloat16),
        cost_estimate=pl.CostEstimate(flops=1 << 22, bytes_accessed=3 << 20, transcendentals=0),
        compiler_params=pltpu.CompilerParams(vmem_limit_bytes=8 << 20),
        name="terms",
    )(received)


def fields_kernel(place, terms, u_rows, *outs):
    sub = outs[0].shape[1]
    core = place[1]
    product = lax.dot_general(
        u_rows[...], terms[...], (((1,), (1,)), ((), ())), preferred_element_type=jnp.float32
    ).astype(jnp.bfloat16)
    for n, out in enumerate(outs):
        base = 2 * sub * n
        out[core] = product[base : base + sub]
        out[1 - core] = product[base + sub : base + 2 * sub]


def fields(place, terms, u_rows, distances):
    rows, depth = u_rows.shape
    wide = terms.shape[0]
    sub = rows // (2 * len(distances))
    return pl.pallas_call(
        fields_kernel,
        in_specs=[pl.BlockSpec(memory_space=pltpu.SMEM), spec(), spec()],
        out_specs=[spec()] * len(distances),
        out_shape=[jax.ShapeDtypeStruct((2, sub, wide), jnp.bfloat16)] * len(distances),
        cost_estimate=pl.CostEstimate(
            flops=2 * rows * depth * wide, bytes_accessed=3 << 20, transcendentals=0
        ),
        compiler_params=pltpu.CompilerParams(vmem_limit_bytes=14 << 20),
    )(place, terms, u_rows)


def halves(terms, kind, period):
    if not terms:
        return None
    half = period // 2
    if len(terms) == 1 or half % 2:
        return direct(terms, kind, period, half + 1)
    even = {n // 2: v for n, v in terms.items() if n % 2 == 0}
    odd = {n: v for n, v in terms.items() if n % 2}
    quarter = half // 2
    a = halves(even, kind, half) if even else [None] * (quarter + 1)
    b = direct(odd, kind, period, quarter + 1)
    out = [None] * (half + 1)
    for t in range(quarter + 1):
        out[t] = plus(a[t], b[t])
        if kind == "cos":
            out[half - t] = plus(a[t], minus(b[t]))
        else:
            out[half - t] = plus(minus(a[t]), b[t])
    return out


def minus(value):
    return None if value is None else ("-", value)


def plus(a, b):
    if a is None or b is None:
        a = b if a is None else a
        if isinstance(a, tuple):
            return -a[1]
        return a
    if isinstance(b, tuple):
        return a - b[1]
    if isinstance(a, tuple):
        return b - a[1]
    return a + b


def direct(terms, kind, period, count):
    out = []
    for t in range(count):
        total = None
        for n, value in terms.items():
            turn = (n * t) % period
            angle = 2.0 * math.pi * turn / period
            weight = math.cos(angle) if kind == "cos" else math.sin(angle)
            if abs(weight) < 1e-9:
                continue
            if abs(weight - 1.0) < 1e-9:
                total = plus(total, value)
            elif abs(weight + 1.0) < 1e-9:
                total = plus(total, minus(value)) if total is not None else -value
            else:
                total = plus(total, value * jnp.float32(weight))
        out.append(total)
    return out


def series_kernel(place, *refs, chips, steps):
    own, swapped = refs[:chips], refs[chips : 2 * chips]
    initial, mutes, taper, focusing, partial, spectra, signal, weighted, total = refs[2 * chips :]
    step = pl.program_id(0)
    chip, core = place[0], place[1]
    trace, rows, focal = initial.shape
    freqs = 2 * chips
    scale = 1.0 / math.sqrt(freqs)
    for d in range(chips):
        source = 2 * lax.rem(chip + chips - d, chips)
        for value, f in ((own[d][...], source + core), (swapped[d][...], source + 1 - core)):
            value = value.astype(jnp.float32) * scale
            spectra[f, 0] = value[:, :focal]
            spectra[f, 1] = value[:, focal:]
    for r in range(rows // 8):
        for q in range(focal // LANES):
            at = (slice(r * 8, (r + 1) * 8), slice(q * LANES, (q + 1) * LANES))
            cosines = halves({f + 1: spectra[(f, 0) + at] for f in range(freqs)}, "cos", trace)
            sines = halves({f + 1: spectra[(f, 1) + at] for f in range(freqs)}, "sin", trace)
            for t in range(trace // 2 + 1):
                signal[(t,) + at] = plus(cosines[t], minus(sines[t]))
                if 0 < t < trace // 2:
                    signal[(trace - t,) + at] = plus(cosines[t], sines[t])
    start = mutes[...]
    weight = taper[...]
    for t in range(trace):
        silenced = jnp.where(t < start, signal[t], 0.0)
        after = (initial[t].astype(jnp.float32) - silenced).astype(jnp.bfloat16)
        focusing[t] = after
        weighted[t] = (after.astype(jnp.float32) * weight).astype(jnp.bfloat16)
    product = lax.dot_general(
        focusing[...].reshape(trace * rows, focal),
        weighted[...].reshape(trace * rows, focal),
        (((0,), (0,)), ((), ())),
        preferred_element_type=jnp.float32,
    )

    @pl.when(step == 0)
    def _():
        total[...] = product

    @pl.when(step > 0)
    def _():
        total[...] += product

    @pl.when(step == steps - 1)
    def _():
        partial[...] = total[...].astype(jnp.bfloat16)


def series_update(place, own, swapped, initial, mutes, taper, rows=16):
    chips = len(own)
    _, trace, sub, focal = initial.shape
    steps = sub // rows
    times = spec((None, trace, rows, focal), lambda s: (0, 0, s, 0))
    return pl.pallas_call(
        functools.partial(series_kernel, chips=chips, steps=steps),
        grid=(steps,),
        in_specs=[pl.BlockSpec(memory_space=pltpu.SMEM)]
        + [spec((None, rows, 2 * focal), lambda s: (0, s, 0))] * chips
        + [spec((rows, 2 * focal), lambda s: (s, 0))] * chips
        + [
            times,
            spec((None, rows, focal), lambda s: (0, s, 0)),
            spec((rows, 1), lambda s: (s, 0)),
        ],
        out_specs=[times, spec((focal, focal), lambda s: (0, 0))],
        scratch_shapes=[
            pltpu.VMEM((2 * chips, 2, rows, focal), jnp.float32),
            pltpu.VMEM((trace, rows, focal), jnp.float32),
            pltpu.VMEM((trace, rows, focal), jnp.bfloat16),
            pltpu.VMEM((focal, focal), jnp.float32),
        ],
        out_shape=[
            jax.ShapeDtypeStruct(initial.shape, jnp.bfloat16),
            jax.ShapeDtypeStruct((focal, focal), jnp.bfloat16),
        ],
        cost_estimate=pl.CostEstimate(
            flops=2 * trace * sub * focal * focal, bytes_accessed=4 << 20, transcendentals=0
        ),
        compiler_params=pltpu.CompilerParams(vmem_limit_bytes=14 << 20),
        name="series",
    )(place, *own, *swapped, initial, mutes, taper)


def swap_cores(values, freq_count):
    return lax.ppermute(values, "freq", [(f, f ^ 1) for f in range(freq_count)])


def shift_chips(values, distance, freq_count):
    pairs = [(f, (f + 2 * distance) % freq_count) for f in range(freq_count)]
    return lax.ppermute(values, "freq", pairs)


def update(focal_field, v_factors, u_factors, ranks, tile_mask, initial_focus, mute_starts, taper):
    tile_count = lax.axis_size("tile")
    freq_count = lax.axis_size("freq")
    me = lax.axis_index("freq")
    chips = freq_count // 2
    place = jnp.stack([me // 2, lax.rem(me, 2)])
    _, _, focal_count = focal_field.shape[1:]
    u_rows = [flatten(place, u_factors[0], distances, chips) for distances in ORDER]
    coeffs = moments(ranks[0, :, 0], tile_mask[0, :, 0], focal_field[0], v_factors[0])
    received = lax.all_to_all(coeffs, "tile", split_axis=0, concat_axis=0, tiled=True)
    terms = rank_terms(received)
    own, swapped = [None] * chips, [None] * chips
    for n, distances in enumerate(ORDER):
        blocks = fields(place, terms, u_rows[n], distances)
        for d, block in zip(distances, blocks):
            own[d] = shift_chips(block, d, freq_count) if d else block
            swapped[d] = swap_cores(own[d][1], freq_count)
    focusing, partial = series_update(
        place, own, swapped, initial_focus, mute_starts, taper[0][:, None]
    )
    shares = lax.all_to_all(partial, "tile", split_axis=0, concat_axis=0, tiled=True)
    trace_length, group_rows = initial_focus.shape[1:3]
    normalizer = 1.0 / float(tile_count * trace_length * group_rows)
    share_rows = focal_count // tile_count
    own_rows = jnp.sum(
        shares.reshape(tile_count, share_rows, focal_count).astype(jnp.float32), axis=0
    )
    return (focusing, (own_rows * normalizer)[None])


def solution(mesh):
    placed = (
        P("freq", "tile", None, None),
        P("freq", None, "tile", None),
        P("freq", "tile", None, None),
        P("freq", None, "tile"),
        P("freq", None, "tile"),
        P("tile", None, "freq", None),
        P("tile", "freq", None),
        P("tile", "freq"),
    )
    return jax.shard_map(
        update,
        mesh=mesh,
        in_specs=placed,
        out_specs=(P("tile", None, "freq", None), P("freq", "tile", None)),
        check_vma=False,
    )
```

```python
import functools
import math

import jax
import jax.numpy as jnp
from jax import lax
from jax.experimental import pallas as pl
from jax.experimental.pallas import tpu as pltpu
from jax.sharding import PartitionSpec as P


LANES = 128
ORDER = ((1, 7), (2, 6), (3, 5), (4, 0))


def spec(block=None, index=None):
    if block is None:
        return pl.BlockSpec(memory_space=pltpu.VMEM)
    return pl.BlockSpec(block, index)


def moments_kernel(ranks, mask, field_hbm, v_hbm, out, field, v_all, field_t, sems):
    rows, _, focal = field.shape
    tiles, _, wide = v_all.shape
    groups = sems.shape[0] - 1
    group = tiles // groups
    fetch = pltpu.make_async_copy(field_hbm, field, sems.at[groups])
    fetch.start()
    fetches = [
        pltpu.make_async_copy(
            v_hbm.at[pl.ds(s * group, group)], v_all.at[pl.ds(s * group, group)], sems.at[s]
        )
        for s in range(groups)
    ]
    for copy in fetches:
        copy.start()
    source = lax.broadcasted_iota(jnp.int32, (2 * LANES, 2 * LANES), 0)
    target = lax.broadcasted_iota(jnp.int32, (2 * LANES, 2 * LANES), 1)
    wanted = 2 * lax.rem(target, LANES) + lax.div(target, LANES)
    apart = (source == wanted).astype(jnp.float32).astype(jnp.bfloat16)
    lane = lax.broadcasted_iota(jnp.int32, (focal, wide), 1)
    sign = jnp.where(lane < wide // 2, -1.0, 1.0)
    level = lax.rem(lane, wide // 2)
    fetch.wait()
    for b in range(rows // LANES):
        for q in range(focal // LANES):
            block = field[b * LANES : (b + 1) * LANES, :, q * LANES : (q + 1) * LANES]
            turned = lax.dot_general(
                block.reshape(2 * LANES, LANES),
                apart,
                (((0,), (0,)), ((), ())),
                preferred_element_type=jnp.float32,
            ).astype(jnp.bfloat16)
            at = slice(b * LANES, (b + 1) * LANES)
            field_t[q * LANES : (q + 1) * LANES, at] = turned[:, :LANES]
            field_t[focal + q * LANES : focal + (q + 1) * LANES, at] = turned[:, LANES:]
    for s in range(groups):
        fetches[s].wait()
        both = jnp.concatenate([v_all[s * group + n] for n in range(group)], axis=1)
        products = jnp.dot(field_t[...], both, preferred_element_type=jnp.float32)
        for n in range(group):
            i = s * group + n
            a = products[:focal, n * wide : (n + 1) * wide]
            b = products[focal:, n * wide : (n + 1) * wide]
            moments = a + sign * pltpu.roll(b, wide // 2, 1)
            kept = jnp.where(mask[i] > 0, ranks[i], 0)
            out[i] = jnp.where(level < kept, moments, 0.0).astype(jnp.bfloat16)


def moments(ranks, mask, field, v_tiles, groups=2):
    tiles, rows, wide = v_tiles.shape
    focal = field.shape[2]
    return pl.pallas_call(
        moments_kernel,
        in_specs=[
            pl.BlockSpec(memory_space=pltpu.SMEM),
            pl.BlockSpec(memory_space=pltpu.SMEM),
            pl.BlockSpec(memory_space=pltpu.HBM),
            pl.BlockSpec(memory_space=pltpu.HBM),
        ],
        out_specs=spec(),
        scratch_shapes=[
            pltpu.VMEM(field.shape, jnp.bfloat16),
            pltpu.VMEM(v_tiles.shape, jnp.bfloat16),
            pltpu.VMEM((2 * focal, rows), jnp.bfloat16),
            pltpu.SemaphoreType.DMA((groups + 1,)),
        ],
        out_shape=jax.ShapeDtypeStruct((tiles, focal, wide), jnp.bfloat16),
        cost_estimate=pl.CostEstimate(
            flops=4 * tiles * rows * wide * focal, bytes_accessed=6 << 20, transcendentals=0
        ),
        compiler_params=pltpu.CompilerParams(vmem_limit_bytes=60 << 20),
        name="moments",
    )(ranks, mask, field, v_tiles)


def flatten_kernel(place, u_tiles, u_rows):
    rows = u_tiles.shape[0]
    u_rows[...] = u_tiles[...].reshape(rows, -1)


def flatten(place, u_tiles, distances, chips):
    rows, tiles, wide = u_tiles.shape
    block = rows // chips

    def source(s, where):
        ahead = sum((jnp.where(s == n, d, 0) for n, d in enumerate(distances)), 0)
        return (lax.rem(where[0] + ahead, chips), 0, 0)

    return pl.pallas_call(
        flatten_kernel,
        grid_spec=pltpu.PrefetchScalarGridSpec(
            num_scalar_prefetch=1,
            grid=(len(distances),),
            in_specs=[spec((block, tiles, wide), source)],
            out_specs=spec((block, tiles * wide), lambda s, where: (s, 0)),
        ),
        out_shape=jax.ShapeDtypeStruct((len(distances) * block, tiles * wide), jnp.bfloat16),
        cost_estimate=pl.CostEstimate(flops=1 << 22, bytes_accessed=8 << 20, transcendentals=0),
        compiler_params=pltpu.CompilerParams(vmem_limit_bytes=60 << 20),
    )(place, u_tiles)


def terms_kernel(received, terms, *, scale):
    tiles, focal, wide = received.shape
    lane = lax.broadcasted_iota(jnp.int32, (focal, wide), 1)
    sign = jnp.where(lane < wide // 2, 1.0, -1.0)
    for j in range(tiles):
        coeffs = received[j].astype(jnp.float32) * scale
        at = slice(j * wide, (j + 1) * wide)
        terms[:focal, at] = (coeffs * sign).astype(jnp.bfloat16)
        terms[focal:, at] = pltpu.roll(coeffs, wide // 2, 1).astype(jnp.bfloat16)


def rank_terms(received, scale):
    tiles, focal, wide = received.shape
    return pl.pallas_call(
        functools.partial(terms_kernel, scale=scale),
        in_specs=[spec()],
        out_specs=spec(),
        out_shape=jax.ShapeDtypeStruct((2 * focal, tiles * wide), jnp.bfloat16),
        cost_estimate=pl.CostEstimate(flops=1 << 22, bytes_accessed=3 << 20, transcendentals=0),
        compiler_params=pltpu.CompilerParams(vmem_limit_bytes=8 << 20),
        name="terms",
    )(received)


def fields_kernel(terms, u_rows, *outs):
    fields_of(terms, u_rows, outs)


def fields_of(terms, u_rows, outs):
    sub = outs[0].shape[1]
    core = lax.rem(lax.axis_index("freq"), 2)
    product = lax.dot_general(
        u_rows[...], terms[...], (((1,), (1,)), ((), ())), preferred_element_type=jnp.float32
    ).astype(jnp.bfloat16)
    for n, out in enumerate(outs):
        base = 2 * sub * n
        out[core] = product[base : base + sub]
        out[1 - core] = product[base + sub : base + 2 * sub]


def fields(terms, u_rows, distances):
    rows, depth = u_rows.shape
    wide = terms.shape[0]
    sub = rows // (2 * len(distances))
    return pl.pallas_call(
        fields_kernel,
        in_specs=[spec(), spec()],
        out_specs=[spec()] * len(distances),
        out_shape=[jax.ShapeDtypeStruct((2, sub, wide), jnp.bfloat16)] * len(distances),
        cost_estimate=pl.CostEstimate(
            flops=2 * rows * depth * wide, bytes_accessed=3 << 20, transcendentals=0
        ),
        compiler_params=pltpu.CompilerParams(vmem_limit_bytes=14 << 20),
    )(terms, u_rows)


def halves(terms, kind, period):
    if not terms:
        return None
    half = period // 2
    if len(terms) == 1 or half % 2:
        return direct(terms, kind, period, half + 1)
    even = {n // 2: v for n, v in terms.items() if n % 2 == 0}
    odd = {n: v for n, v in terms.items() if n % 2}
    quarter = half // 2
    a = halves(even, kind, half) if even else [None] * (quarter + 1)
    b = direct(odd, kind, period, quarter + 1)
    out = [None] * (half + 1)
    for t in range(quarter + 1):
        out[t] = plus(a[t], b[t])
        if kind == "cos":
            out[half - t] = plus(a[t], minus(b[t]))
        else:
            out[half - t] = plus(minus(a[t]), b[t])
    return out


def minus(value):
    return None if value is None else ("-", value)


def plus(a, b):
    if a is None or b is None:
        a = b if a is None else a
        if isinstance(a, tuple):
            return -a[1]
        return a
    if isinstance(b, tuple):
        return a - b[1]
    if isinstance(a, tuple):
        return b - a[1]
    return a + b


def direct(terms, kind, period, count):
    out = []
    for t in range(count):
        total = None
        for n, value in terms.items():
            turn = (n * t) % period
            angle = 2.0 * math.pi * turn / period
            weight = math.cos(angle) if kind == "cos" else math.sin(angle)
            if abs(weight) < 1e-9:
                continue
            if abs(weight - 1.0) < 1e-9:
                total = plus(total, value)
            elif abs(weight + 1.0) < 1e-9:
                total = plus(total, minus(value)) if total is not None else -value
            else:
                total = plus(total, value * jnp.float32(weight))
        out.append(total)
    return out


def series_kernel(*refs, chips, steps, scale):
    own, swapped = refs[:chips], refs[chips : 2 * chips]
    initial, mutes, taper, focusing, partial, spectra, signal, weighted, total = refs[2 * chips :]
    step = pl.program_id(0)
    me = lax.axis_index("freq")
    chip, core = lax.div(me, 2), lax.rem(me, 2)
    trace, rows, focal = initial.shape
    freqs = 2 * chips
    for d in range(chips):
        source = 2 * lax.rem(chip + chips - d, chips)
        for value, f in ((own[d][...], source + core), (swapped[d][...], source + 1 - core)):
            value = value.astype(jnp.float32)
            spectra[f, 0] = value[:, :focal]
            spectra[f, 1] = value[:, focal:]
    for r in range(rows // 8):
        for q in range(focal // LANES):
            at = (slice(r * 8, (r + 1) * 8), slice(q * LANES, (q + 1) * LANES))
            cosines = halves({f + 1: spectra[(f, 0) + at] for f in range(freqs)}, "cos", trace)
            sines = halves({f + 1: spectra[(f, 1) + at] for f in range(freqs)}, "sin", trace)
            for t in range(trace // 2 + 1):
                signal[(t,) + at] = plus(cosines[t], minus(sines[t]))
                if 0 < t < trace // 2:
                    signal[(trace - t,) + at] = plus(cosines[t], sines[t])
    start = mutes[...]
    weight = taper[...]
    for t in range(trace):
        silenced = jnp.where(t < start, signal[t], 0.0)
        after = (initial[t].astype(jnp.float32) - silenced).astype(jnp.bfloat16)
        focusing[t] = after
        weighted[t] = (after.astype(jnp.float32) * weight).astype(jnp.bfloat16)
    product = lax.dot_general(
        focusing[...].reshape(trace * rows, focal),
        weighted[...].reshape(trace * rows, focal),
        (((0,), (0,)), ((), ())),
        preferred_element_type=jnp.float32,
    )

    @pl.when(step == 0)
    def _():
        total[...] = product

    @pl.when(step > 0)
    def _():
        total[...] += product

    @pl.when(step == steps - 1)
    def _():
        partial[...] = (total[...] * scale).astype(jnp.bfloat16)


def series_update(own, swapped, initial, mutes, taper, scale, rows=16):
    chips = len(own)
    _, trace, sub, focal = initial.shape
    steps = sub // rows
    times = spec((None, trace, rows, focal), lambda s: (0, 0, s, 0))
    return pl.pallas_call(
        functools.partial(series_kernel, chips=chips, steps=steps, scale=scale),
        grid=(steps,),
        in_specs=[spec((None, rows, 2 * focal), lambda s: (0, s, 0))] * chips
        + [spec((rows, 2 * focal), lambda s: (s, 0))] * chips
        + [
            times,
            spec((None, rows, focal), lambda s: (0, s, 0)),
            spec((rows, 1), lambda s: (s, 0)),
        ],
        out_specs=[times, spec((focal, focal), lambda s: (0, 0))],
        scratch_shapes=[
            pltpu.VMEM((2 * chips, 2, rows, focal), jnp.float32),
            pltpu.VMEM((trace, rows, focal), jnp.float32),
            pltpu.VMEM((trace, rows, focal), jnp.bfloat16),
            pltpu.VMEM((focal, focal), jnp.float32),
        ],
        out_shape=[
            jax.ShapeDtypeStruct(initial.shape, jnp.bfloat16),
            jax.ShapeDtypeStruct((focal, focal), jnp.bfloat16),
        ],
        cost_estimate=pl.CostEstimate(
            flops=2 * trace * sub * focal * focal, bytes_accessed=4 << 20, transcendentals=0
        ),
        compiler_params=pltpu.CompilerParams(vmem_limit_bytes=14 << 20),
        name="series",
    )(*own, *swapped, initial, mutes, taper)


def swap_cores(values, freq_count):
    return lax.ppermute(values, "freq", [(f, f ^ 1) for f in range(freq_count)])


def shift_chips(values, distance, freq_count):
    pairs = [(f, (f + 2 * distance) % freq_count) for f in range(freq_count)]
    return lax.ppermute(values, "freq", pairs)


def update(focal_field, v_factors, u_factors, ranks, tile_mask, initial_focus, mute_starts, taper):
    tile_count = lax.axis_size("tile")
    freq_count = lax.axis_size("freq")
    me = lax.axis_index("freq")
    chips = freq_count // 2
    place = jnp.stack([me // 2, lax.rem(me, 2)])
    _, _, focal_count = focal_field.shape[1:]
    u_rows = [flatten(place, u_factors[0], distances, chips) for distances in ORDER]
    coeffs = moments(ranks[0, :, 0], tile_mask[0, :, 0], focal_field[0], v_factors[0])
    received = lax.all_to_all(coeffs, "tile", split_axis=0, concat_axis=0, tiled=True)
    terms = rank_terms(received, 1.0 / math.sqrt(freq_count))
    own, swapped = [None] * chips, [None] * chips
    for n, distances in enumerate(ORDER):
        blocks = fields(terms, u_rows[n], distances)
        for d, block in zip(distances, blocks):
            own[d] = shift_chips(block, d, freq_count) if d else block
            swapped[d] = swap_cores(own[d][1], freq_count)
    trace_length, group_rows = initial_focus.shape[1:3]
    normalizer = 1.0 / float(tile_count * trace_length * group_rows)
    focusing, partial = series_update(
        own, swapped, initial_focus, mute_starts, taper[0][:, None], normalizer
    )
    shares = lax.all_to_all(partial, "tile", split_axis=0, concat_axis=0, tiled=True)
    share_rows = focal_count // tile_count
    shares = shares.reshape(tile_count, 1, share_rows, focal_count)
    return (focusing, jnp.sum(shares.astype(jnp.float32), axis=0))


def solution(mesh):
    placed = (
        P("freq", "tile", None, None),
        P("freq", None, "tile", None),
        P("freq", "tile", None, None),
        P("freq", None, "tile"),
        P("freq", None, "tile"),
        P("tile", None, "freq", None),
        P("tile", "freq", None),
        P("tile", "freq"),
    )
    return jax.shard_map(
        update,
        mesh=mesh,
        in_specs=placed,
        out_specs=(P("tile", None, "freq", None), P("freq", "tile", None)),
        check_vma=False,
    )
```

```python
import functools
import math

import jax
import jax.numpy as jnp
from jax import lax
from jax.experimental import pallas as pl
from jax.experimental.pallas import tpu as pltpu
from jax.sharding import PartitionSpec as P


LANES = 128
ORDER = ((2, 6), (4, 0), (3, 5), (1, 7))


def spec(block=None, index=None):
    if block is None:
        return pl.BlockSpec(memory_space=pltpu.VMEM)
    return pl.BlockSpec(block, index)


def moments_kernel(ranks, mask, field_hbm, v_hbm, out, field, v_all, field_t, sems):
    rows, _, focal = field.shape
    tiles, _, wide = v_all.shape
    groups = sems.shape[0] - 1
    group = tiles // groups
    fetch = pltpu.make_async_copy(field_hbm, field, sems.at[groups])
    fetch.start()
    fetches = [
        pltpu.make_async_copy(
            v_hbm.at[pl.ds(s * group, group)], v_all.at[pl.ds(s * group, group)], sems.at[s]
        )
        for s in range(groups)
    ]
    for copy in fetches:
        copy.start()
    source = lax.broadcasted_iota(jnp.int32, (2 * LANES, 2 * LANES), 0)
    target = lax.broadcasted_iota(jnp.int32, (2 * LANES, 2 * LANES), 1)
    wanted = 2 * lax.rem(target, LANES) + lax.div(target, LANES)
    apart = (source == wanted).astype(jnp.float32).astype(jnp.bfloat16)
    lane = lax.broadcasted_iota(jnp.int32, (focal, wide), 1)
    sign = jnp.where(lane < wide // 2, -1.0, 1.0)
    level = lax.rem(lane, wide // 2)
    fetch.wait()
    for b in range(rows // LANES):
        for q in range(focal // LANES):
            block = field[b * LANES : (b + 1) * LANES, :, q * LANES : (q + 1) * LANES]
            turned = lax.dot_general(
                block.reshape(2 * LANES, LANES),
                apart,
                (((0,), (0,)), ((), ())),
                preferred_element_type=jnp.float32,
            ).astype(jnp.bfloat16)
            at = slice(b * LANES, (b + 1) * LANES)
            field_t[q * LANES : (q + 1) * LANES, at] = turned[:, :LANES]
            field_t[focal + q * LANES : focal + (q + 1) * LANES, at] = turned[:, LANES:]
    for s in range(groups):
        fetches[s].wait()
        both = jnp.concatenate([v_all[s * group + n] for n in range(group)], axis=1)
        products = jnp.dot(field_t[...], both, preferred_element_type=jnp.float32)
        for n in range(group):
            i = s * group + n
            a = products[:focal, n * wide : (n + 1) * wide]
            b = products[focal:, n * wide : (n + 1) * wide]
            moments = a + sign * pltpu.roll(b, wide // 2, 1)
            kept = jnp.where(mask[i] > 0, ranks[i], 0)
            out[i] = jnp.where(level < kept, moments, 0.0).astype(jnp.bfloat16)


def moments(ranks, mask, field, v_tiles, groups=2):
    tiles, rows, wide = v_tiles.shape
    focal = field.shape[2]
    return pl.pallas_call(
        moments_kernel,
        in_specs=[
            pl.BlockSpec(memory_space=pltpu.SMEM),
            pl.BlockSpec(memory_space=pltpu.SMEM),
            pl.BlockSpec(memory_space=pltpu.HBM),
            pl.BlockSpec(memory_space=pltpu.HBM),
        ],
        out_specs=spec(),
        scratch_shapes=[
            pltpu.VMEM(field.shape, jnp.bfloat16),
            pltpu.VMEM(v_tiles.shape, jnp.bfloat16),
            pltpu.VMEM((2 * focal, rows), jnp.bfloat16),
            pltpu.SemaphoreType.DMA((groups + 1,)),
        ],
        out_shape=jax.ShapeDtypeStruct((tiles, focal, wide), jnp.bfloat16),
        cost_estimate=pl.CostEstimate(
            flops=4 * tiles * rows * wide * focal, bytes_accessed=6 << 20, transcendentals=0
        ),
        compiler_params=pltpu.CompilerParams(vmem_limit_bytes=60 << 20),
        name="moments",
    )(ranks, mask, field, v_tiles)


def flatten_kernel(place, u_tiles, u_rows):
    rows = u_tiles.shape[0]
    u_rows[...] = u_tiles[...].reshape(rows, -1)


def flatten(place, u_tiles, distances, chips):
    rows, tiles, wide = u_tiles.shape
    block = rows // chips

    def source(s, where):
        ahead = sum((jnp.where(s == n, d, 0) for n, d in enumerate(distances)), 0)
        return (lax.rem(where[0] + ahead, chips), 0, 0)

    return pl.pallas_call(
        flatten_kernel,
        grid_spec=pltpu.PrefetchScalarGridSpec(
            num_scalar_prefetch=1,
            grid=(len(distances),),
            in_specs=[spec((block, tiles, wide), source)],
            out_specs=spec((block, tiles * wide), lambda s, where: (s, 0)),
        ),
        out_shape=jax.ShapeDtypeStruct((len(distances) * block, tiles * wide), jnp.bfloat16),
        cost_estimate=pl.CostEstimate(flops=1 << 22, bytes_accessed=8 << 20, transcendentals=0),
        compiler_params=pltpu.CompilerParams(vmem_limit_bytes=60 << 20),
    )(place, u_tiles)


def terms_kernel(received, terms, *, scale):
    tiles, focal, wide = received.shape
    lane = lax.broadcasted_iota(jnp.int32, (focal, wide), 1)
    sign = jnp.where(lane < wide // 2, 1.0, -1.0)
    for j in range(tiles):
        coeffs = received[j].astype(jnp.float32) * scale
        at = slice(j * wide, (j + 1) * wide)
        terms[:focal, at] = (coeffs * sign).astype(jnp.bfloat16)
        terms[focal:, at] = pltpu.roll(coeffs, wide // 2, 1).astype(jnp.bfloat16)


def rank_terms(received, scale):
    tiles, focal, wide = received.shape
    return pl.pallas_call(
        functools.partial(terms_kernel, scale=scale),
        in_specs=[spec()],
        out_specs=spec(),
        out_shape=jax.ShapeDtypeStruct((2 * focal, tiles * wide), jnp.bfloat16),
        cost_estimate=pl.CostEstimate(flops=1 << 22, bytes_accessed=3 << 20, transcendentals=0),
        compiler_params=pltpu.CompilerParams(vmem_limit_bytes=8 << 20),
        name="terms",
    )(received)


def fields_kernel(terms, u_rows, *outs):
    fields_of(terms, u_rows, outs)


def fields_of(terms, u_rows, outs):
    sub = outs[0].shape[1]
    core = lax.rem(lax.axis_index("freq"), 2)
    product = lax.dot_general(
        u_rows[...], terms[...], (((1,), (1,)), ((), ())), preferred_element_type=jnp.float32
    ).astype(jnp.bfloat16)
    for n, out in enumerate(outs):
        base = 2 * sub * n
        out[core] = product[base : base + sub]
        out[1 - core] = product[base + sub : base + 2 * sub]


def fields(terms, u_rows, distances):
    rows, depth = u_rows.shape
    wide = terms.shape[0]
    sub = rows // (2 * len(distances))
    return pl.pallas_call(
        fields_kernel,
        in_specs=[spec(), spec()],
        out_specs=[spec()] * len(distances),
        out_shape=[jax.ShapeDtypeStruct((2, sub, wide), jnp.bfloat16)] * len(distances),
        cost_estimate=pl.CostEstimate(
            flops=2 * rows * depth * wide, bytes_accessed=3 << 20, transcendentals=0
        ),
        compiler_params=pltpu.CompilerParams(vmem_limit_bytes=14 << 20),
    )(terms, u_rows)


def halves(terms, kind, period):
    if not terms:
        return None
    half = period // 2
    if len(terms) == 1 or half % 2:
        return direct(terms, kind, period, half + 1)
    even = {n // 2: v for n, v in terms.items() if n % 2 == 0}
    odd = {n: v for n, v in terms.items() if n % 2}
    quarter = half // 2
    a = halves(even, kind, half) if even else [None] * (quarter + 1)
    b = direct(odd, kind, period, quarter + 1)
    out = [None] * (half + 1)
    for t in range(quarter + 1):
        out[t] = plus(a[t], b[t])
        if kind == "cos":
            out[half - t] = plus(a[t], minus(b[t]))
        else:
            out[half - t] = plus(minus(a[t]), b[t])
    return out


def minus(value):
    return None if value is None else ("-", value)


def plus(a, b):
    if a is None or b is None:
        a = b if a is None else a
        if isinstance(a, tuple):
            return -a[1]
        return a
    if isinstance(b, tuple):
        return a - b[1]
    if isinstance(a, tuple):
        return b - a[1]
    return a + b


def direct(terms, kind, period, count):
    out = []
    for t in range(count):
        total = None
        for n, value in terms.items():
            turn = (n * t) % period
            angle = 2.0 * math.pi * turn / period
            weight = math.cos(angle) if kind == "cos" else math.sin(angle)
            if abs(weight) < 1e-9:
                continue
            if abs(weight - 1.0) < 1e-9:
                total = plus(total, value)
            elif abs(weight + 1.0) < 1e-9:
                total = plus(total, minus(value)) if total is not None else -value
            else:
                total = plus(total, value * jnp.float32(weight))
        out.append(total)
    return out


def series_kernel(*refs, chips, steps, scale):
    groups = len(ORDER)
    own = refs[:chips]
    swapped = [None] * chips
    for group, distances in zip(refs[chips : chips + groups], ORDER):
        for n, d in enumerate(distances):
            swapped[d] = group.at[n]
    initial, mutes, taper, focusing, partial, spectra, signal, weighted, total = refs[chips + groups :]
    step = pl.program_id(0)
    me = lax.axis_index("freq")
    chip, core = lax.div(me, 2), lax.rem(me, 2)
    trace, rows, focal = initial.shape
    freqs = 2 * chips
    for d in range(chips):
        source = 2 * lax.rem(chip + chips - d, chips)
        for value, f in ((own[d][...], source + core), (swapped[d][...], source + 1 - core)):
            value = value.astype(jnp.float32)
            spectra[f, 0] = value[:, :focal]
            spectra[f, 1] = value[:, focal:]
    for r in range(rows // 8):
        for q in range(focal // LANES):
            at = (slice(r * 8, (r + 1) * 8), slice(q * LANES, (q + 1) * LANES))
            cosines = halves({f + 1: spectra[(f, 0) + at] for f in range(freqs)}, "cos", trace)
            sines = halves({f + 1: spectra[(f, 1) + at] for f in range(freqs)}, "sin", trace)
            for t in range(trace // 2 + 1):
                signal[(t,) + at] = plus(cosines[t], minus(sines[t]))
                if 0 < t < trace // 2:
                    signal[(trace - t,) + at] = plus(cosines[t], sines[t])
    start = mutes[...]
    weight = taper[...]
    for t in range(trace):
        silenced = jnp.where(t < start, signal[t], 0.0)
        after = (initial[t].astype(jnp.float32) - silenced).astype(jnp.bfloat16)
        focusing[t] = after
        weighted[t] = (after.astype(jnp.float32) * weight).astype(jnp.bfloat16)
    product = lax.dot_general(
        focusing[...].reshape(trace * rows, focal),
        weighted[...].reshape(trace * rows, focal),
        (((0,), (0,)), ((), ())),
        preferred_element_type=jnp.float32,
    )

    @pl.when(step == 0)
    def _():
        total[...] = product

    @pl.when(step > 0)
    def _():
        total[...] += product

    @pl.when(step == steps - 1)
    def _():
        partial[...] = (total[...] * scale).astype(jnp.bfloat16)


def series_update(own, swapped, initial, mutes, taper, scale, rows=64):
    chips = len(own)
    _, trace, sub, focal = initial.shape
    steps = sub // rows
    times = spec((None, trace, rows, focal), lambda s: (0, 0, s, 0))
    return pl.pallas_call(
        functools.partial(series_kernel, chips=chips, steps=steps, scale=scale),
        grid=(steps,),
        in_specs=[spec((None, rows, 2 * focal), lambda s: (0, s, 0))] * chips
        + [spec((block.shape[0], rows, 2 * focal), lambda s: (0, s, 0)) for block in swapped]
        + [
            times,
            spec((None, rows, focal), lambda s: (0, s, 0)),
            spec((rows, 1), lambda s: (s, 0)),
        ],
        out_specs=[times, spec((focal, focal), lambda s: (0, 0))],
        scratch_shapes=[
            pltpu.VMEM((2 * chips, 2, rows, focal), jnp.float32),
            pltpu.VMEM((trace, rows, focal), jnp.float32),
            pltpu.VMEM((trace, rows, focal), jnp.bfloat16),
            pltpu.VMEM((focal, focal), jnp.float32),
        ],
        out_shape=[
            jax.ShapeDtypeStruct(initial.shape, jnp.bfloat16),
            jax.ShapeDtypeStruct((focal, focal), jnp.bfloat16),
        ],
        cost_estimate=pl.CostEstimate(
            flops=2 * trace * sub * focal * focal, bytes_accessed=4 << 20, transcendentals=0
        ),
        compiler_params=pltpu.CompilerParams(vmem_limit_bytes=14 << 20),
        name="series",
    )(*own, *swapped, initial, mutes, taper)


def second_kernel(*refs):
    for n, ref in enumerate(refs[:-1]):
        refs[-1][n] = ref[1]


def second_parts(blocks):
    shape = (len(blocks),) + blocks[0].shape[1:]
    return pl.pallas_call(
        second_kernel,
        in_specs=[spec()] * len(blocks),
        out_specs=spec(),
        out_shape=jax.ShapeDtypeStruct(shape, blocks[0].dtype),
        cost_estimate=pl.CostEstimate(flops=0, bytes_accessed=1 << 18, transcendentals=0),
        compiler_params=pltpu.CompilerParams(vmem_limit_bytes=2 << 20),
        name="second",
    )(*blocks)


def swap_cores(values, freq_count):
    return lax.ppermute(values, "freq", [(f, f ^ 1) for f in range(freq_count)])


def shift_chips(values, distance, freq_count):
    pairs = [(f, (f + 2 * distance) % freq_count) for f in range(freq_count)]
    return lax.ppermute(values, "freq", pairs)


def update(focal_field, v_factors, u_factors, ranks, tile_mask, initial_focus, mute_starts, taper):
    tile_count = lax.axis_size("tile")
    freq_count = lax.axis_size("freq")
    me = lax.axis_index("freq")
    chips = freq_count // 2
    place = jnp.stack([me // 2, lax.rem(me, 2)])
    _, _, focal_count = focal_field.shape[1:]
    u_rows = [flatten(place, u_factors[0], distances, chips) for distances in ORDER]
    coeffs = moments(ranks[0, :, 0], tile_mask[0, :, 0], focal_field[0], v_factors[0])
    received = lax.all_to_all(coeffs, "tile", split_axis=0, concat_axis=0, tiled=True)
    terms = rank_terms(received, 1.0 / math.sqrt(freq_count))
    own, swapped = [None] * chips, []
    for n, distances in enumerate(ORDER):
        blocks = fields(terms, u_rows[n], distances)
        for d, block in zip(distances, blocks):
            own[d] = shift_chips(block, d, freq_count) if d else block
        swapped.append(swap_cores(second_parts([own[d] for d in distances]), freq_count))
    trace_length, group_rows = initial_focus.shape[1:3]
    normalizer = 1.0 / float(tile_count * trace_length * group_rows)
    focusing, partial = series_update(
        own, swapped, initial_focus, mute_starts, taper[0][:, None], normalizer
    )
    shares = lax.all_to_all(partial, "tile", split_axis=0, concat_axis=0, tiled=True)
    share_rows = focal_count // tile_count
    shares = shares.reshape(tile_count, 1, share_rows, focal_count)
    return (focusing, jnp.sum(shares.astype(jnp.float32), axis=0))


def solution(mesh):
    placed = (
        P("freq", "tile", None, None),
        P("freq", None, "tile", None),
        P("freq", "tile", None, None),
        P("freq", None, "tile"),
        P("freq", None, "tile"),
        P("tile", None, "freq", None),
        P("tile", "freq", None),
        P("tile", "freq"),
    )
    return jax.shard_map(
        update,
        mesh=mesh,
        in_specs=placed,
        out_specs=(P("tile", None, "freq", None), P("freq", "tile", None)),
        check_vma=False,
    )
```

```python
import functools
import math

import jax
import jax.numpy as jnp
from jax import lax
from jax.experimental import pallas as pl
from jax.experimental.pallas import tpu as pltpu
from jax.sharding import PartitionSpec as P


LANES = 128
ORDER = ((2, 6), (3, 5), (4, 0), (1, 7))


def spec(block=None, index=None):
    if block is None:
        return pl.BlockSpec(memory_space=pltpu.VMEM)
    return pl.BlockSpec(block, index)


def moments_kernel(ranks, mask, field_hbm, v_hbm, out_hbm, field, v_all, field_t, out, sems):
    rows, _, focal = field.shape
    tiles, _, wide = v_all.shape
    groups = (sems.shape[0] - 1) // 2
    group = tiles // groups
    fetch = pltpu.make_async_copy(field_hbm, field, sems.at[2 * groups])
    fetch.start()
    fetches = [
        pltpu.make_async_copy(
            v_hbm.at[pl.ds(s * group, group)], v_all.at[pl.ds(s * group, group)], sems.at[s]
        )
        for s in range(groups)
    ]
    fetches[0].start()
    source = lax.broadcasted_iota(jnp.int32, (2 * LANES, 2 * LANES), 0)
    target = lax.broadcasted_iota(jnp.int32, (2 * LANES, 2 * LANES), 1)
    wanted = 2 * lax.rem(target, LANES) + lax.div(target, LANES)
    apart = (source == wanted).astype(jnp.float32).astype(jnp.bfloat16)
    lane = lax.broadcasted_iota(jnp.int32, (focal, wide), 1)
    sign = jnp.where(lane < wide // 2, -1.0, 1.0)
    level = lax.rem(lane, wide // 2)
    fetch.wait()
    for copy in fetches[1:]:
        copy.start()
    for b in range(rows // LANES):
        for q in range(focal // LANES):
            block = field[b * LANES : (b + 1) * LANES, :, q * LANES : (q + 1) * LANES]
            turned = lax.dot_general(
                block.reshape(2 * LANES, LANES),
                apart,
                (((0,), (0,)), ((), ())),
                preferred_element_type=jnp.float32,
            ).astype(jnp.bfloat16)
            at = slice(b * LANES, (b + 1) * LANES)
            field_t[q * LANES : (q + 1) * LANES, at] = turned[:, :LANES]
            field_t[focal + q * LANES : focal + (q + 1) * LANES, at] = turned[:, LANES:]
    puts = []
    for s in range(groups):
        fetches[s].wait()
        both = jnp.concatenate([v_all[s * group + n] for n in range(group)], axis=1)
        products = jnp.dot(field_t[...], both, preferred_element_type=jnp.float32)
        for n in range(group):
            i = s * group + n
            a = products[:focal, n * wide : (n + 1) * wide]
            b = products[focal:, n * wide : (n + 1) * wide]
            moments = a + sign * pltpu.roll(b, wide // 2, 1)
            kept = jnp.where(mask[i] > 0, ranks[i], 0)
            out[i] = jnp.where(level < kept, moments, 0.0).astype(jnp.bfloat16)
        at = pl.ds(s * group, group)
        puts.append(pltpu.make_async_copy(out.at[at], out_hbm.at[at], sems.at[groups + s]))
        puts[-1].start()
    for copy in puts:
        copy.wait()


def moments(ranks, mask, field, v_tiles, groups=2):
    tiles, rows, wide = v_tiles.shape
    focal = field.shape[2]
    return pl.pallas_call(
        moments_kernel,
        in_specs=[
            pl.BlockSpec(memory_space=pltpu.SMEM),
            pl.BlockSpec(memory_space=pltpu.SMEM),
            pl.BlockSpec(memory_space=pltpu.HBM),
            pl.BlockSpec(memory_space=pltpu.HBM),
        ],
        out_specs=pl.BlockSpec(memory_space=pltpu.HBM),
        scratch_shapes=[
            pltpu.VMEM(field.shape, jnp.bfloat16),
            pltpu.VMEM(v_tiles.shape, jnp.bfloat16),
            pltpu.VMEM((2 * focal, rows), jnp.bfloat16),
            pltpu.VMEM((tiles, focal, wide), jnp.bfloat16),
            pltpu.SemaphoreType.DMA((2 * groups + 1,)),
        ],
        out_shape=jax.ShapeDtypeStruct((tiles, focal, wide), jnp.bfloat16),
        cost_estimate=pl.CostEstimate(
            flops=4 * tiles * rows * wide * focal, bytes_accessed=6 << 20, transcendentals=0
        ),
        compiler_params=pltpu.CompilerParams(vmem_limit_bytes=60 << 20),
        name="moments",
    )(ranks, mask, field, v_tiles)


def flatten_kernel(place, u_tiles, u_rows):
    rows = u_tiles.shape[0]
    u_rows[...] = u_tiles[...].reshape(rows, -1)


def flatten(place, u_tiles, distances, chips):
    rows, tiles, wide = u_tiles.shape
    block = rows // chips

    def source(s, where):
        ahead = sum((jnp.where(s == n, d, 0) for n, d in enumerate(distances)), 0)
        return (lax.rem(where[0] + ahead, chips), 0, 0)

    return pl.pallas_call(
        flatten_kernel,
        grid_spec=pltpu.PrefetchScalarGridSpec(
            num_scalar_prefetch=1,
            grid=(len(distances),),
            in_specs=[spec((block, tiles, wide), source)],
            out_specs=spec((block, tiles * wide), lambda s, where: (s, 0)),
        ),
        out_shape=jax.ShapeDtypeStruct((len(distances) * block, tiles * wide), jnp.bfloat16),
        cost_estimate=pl.CostEstimate(flops=1 << 22, bytes_accessed=8 << 20, transcendentals=0),
        compiler_params=pltpu.CompilerParams(vmem_limit_bytes=60 << 20),
    )(place, u_tiles)


def terms_kernel(received, u_in, terms, u_out, *, scale):
    tiles, focal, wide = received.shape
    lane = lax.broadcasted_iota(jnp.int32, (focal, wide), 1)
    sign = jnp.where(lane < wide // 2, 1.0, -1.0)
    for j in range(tiles):
        coeffs = received[j].astype(jnp.float32) * scale
        at = slice(j * wide, (j + 1) * wide)
        terms[:focal, at] = (coeffs * sign).astype(jnp.bfloat16)
        terms[focal:, at] = pltpu.roll(coeffs, wide // 2, 1).astype(jnp.bfloat16)


def rank_terms(received, u_rows, scale):
    tiles, focal, wide = received.shape
    return pl.pallas_call(
        functools.partial(terms_kernel, scale=scale),
        in_specs=[spec(), pl.BlockSpec(memory_space=pl.ANY)],
        out_specs=[spec(), pl.BlockSpec(memory_space=pl.ANY)],
        out_shape=[
            jax.ShapeDtypeStruct((2 * focal, tiles * wide), jnp.bfloat16),
            jax.ShapeDtypeStruct(u_rows.shape, u_rows.dtype),
        ],
        input_output_aliases={1: 1},
        cost_estimate=pl.CostEstimate(flops=1 << 22, bytes_accessed=3 << 20, transcendentals=0),
        compiler_params=pltpu.CompilerParams(vmem_limit_bytes=8 << 20),
        name="terms",
    )(received, u_rows)


def fields_kernel(terms, u_rows, *outs):
    fields_of(terms, u_rows, outs)


def fields_of(terms, u_rows, outs):
    sub = outs[0].shape[1]
    core = lax.rem(lax.axis_index("freq"), 2)
    product = lax.dot_general(
        u_rows[...], terms[...], (((1,), (1,)), ((), ())), preferred_element_type=jnp.float32
    ).astype(jnp.bfloat16)
    for n, out in enumerate(outs):
        base = 2 * sub * n
        out[core] = product[base : base + sub]
        out[1 - core] = product[base + sub : base + 2 * sub]


def fields(terms, u_rows, distances):
    rows, depth = u_rows.shape
    wide = terms.shape[0]
    sub = rows // (2 * len(distances))
    return pl.pallas_call(
        fields_kernel,
        in_specs=[spec(), spec()],
        out_specs=[spec()] * len(distances),
        out_shape=[jax.ShapeDtypeStruct((2, sub, wide), jnp.bfloat16)] * len(distances),
        cost_estimate=pl.CostEstimate(
            flops=2 * rows * depth * wide, bytes_accessed=3 << 20, transcendentals=0
        ),
        compiler_params=pltpu.CompilerParams(vmem_limit_bytes=14 << 20),
    )(terms, u_rows)


def halves(terms, kind, period):
    if not terms:
        return None
    half = period // 2
    if len(terms) == 1 or half % 2:
        return direct(terms, kind, period, half + 1)
    even = {n // 2: v for n, v in terms.items() if n % 2 == 0}
    odd = {n: v for n, v in terms.items() if n % 2}
    quarter = half // 2
    a = halves(even, kind, half) if even else [None] * (quarter + 1)
    b = direct(odd, kind, period, quarter + 1)
    out = [None] * (half + 1)
    for t in range(quarter + 1):
        out[t] = plus(a[t], b[t])
        if kind == "cos":
            out[half - t] = plus(a[t], minus(b[t]))
        else:
            out[half - t] = plus(minus(a[t]), b[t])
    return out


def minus(value):
    return None if value is None else ("-", value)


def plus(a, b):
    if a is None or b is None:
        a = b if a is None else a
        if isinstance(a, tuple):
            return -a[1]
        return a
    if isinstance(b, tuple):
        return a - b[1]
    if isinstance(a, tuple):
        return b - a[1]
    return a + b


def direct(terms, kind, period, count):
    out = []
    for t in range(count):
        total = None
        for n, value in terms.items():
            turn = (n * t) % period
            angle = 2.0 * math.pi * turn / period
            weight = math.cos(angle) if kind == "cos" else math.sin(angle)
            if abs(weight) < 1e-9:
                continue
            if abs(weight - 1.0) < 1e-9:
                total = plus(total, value)
            elif abs(weight + 1.0) < 1e-9:
                total = plus(total, minus(value)) if total is not None else -value
            else:
                total = plus(total, value * jnp.float32(weight))
        out.append(total)
    return out


def series_kernel(*refs, chips, steps, scale):
    groups = len(ORDER)
    own = refs[:chips]
    swapped = [None] * chips
    for group, distances in zip(refs[chips : chips + groups], ORDER):
        for n, d in enumerate(distances):
            swapped[d] = group.at[n]
    initial, mutes, taper, focusing, partial, spectra, signal, weighted, total = refs[chips + groups :]
    step = pl.program_id(0)
    me = lax.axis_index("freq")
    chip, core = lax.div(me, 2), lax.rem(me, 2)
    trace, rows, focal = initial.shape
    freqs = 2 * chips
    for d in range(chips):
        source = 2 * lax.rem(chip + chips - d, chips)
        for value, f in ((own[d][...], source + core), (swapped[d][...], source + 1 - core)):
            value = value.astype(jnp.float32)
            spectra[f, 0] = value[:, :focal]
            spectra[f, 1] = value[:, focal:]
    for r in range(rows // 8):
        for q in range(focal // LANES):
            at = (slice(r * 8, (r + 1) * 8), slice(q * LANES, (q + 1) * LANES))
            cosines = halves({f + 1: spectra[(f, 0) + at] for f in range(freqs)}, "cos", trace)
            sines = halves({f + 1: spectra[(f, 1) + at] for f in range(freqs)}, "sin", trace)
            for t in range(trace // 2 + 1):
                signal[(t,) + at] = plus(cosines[t], minus(sines[t]))
                if 0 < t < trace // 2:
                    signal[(trace - t,) + at] = plus(cosines[t], sines[t])
    start = mutes[...]
    weight = taper[...]
    for t in range(trace):
        silenced = jnp.where(t < start, signal[t], 0.0)
        after = (initial[t].astype(jnp.float32) - silenced).astype(jnp.bfloat16)
        focusing[t] = after
        weighted[t] = (after.astype(jnp.float32) * weight).astype(jnp.bfloat16)
    product = lax.dot_general(
        focusing[...].reshape(trace * rows, focal),
        weighted[...].reshape(trace * rows, focal),
        (((0,), (0,)), ((), ())),
        preferred_element_type=jnp.float32,
    )

    @pl.when(step == 0)
    def _():
        total[...] = product

    @pl.when(step > 0)
    def _():
        total[...] += product

    @pl.when(step == steps - 1)
    def _():
        partial[...] = (total[...] * scale).astype(jnp.bfloat16)


def series_update(own, swapped, initial, mutes, taper, scale, rows=64):
    chips = len(own)
    _, trace, sub, focal = initial.shape
    steps = sub // rows
    times = spec((None, trace, rows, focal), lambda s: (0, 0, s, 0))
    return pl.pallas_call(
        functools.partial(series_kernel, chips=chips, steps=steps, scale=scale),
        grid=(steps,),
        in_specs=[spec((None, rows, 2 * focal), lambda s: (0, s, 0))] * chips
        + [spec((block.shape[0], rows, 2 * focal), lambda s: (0, s, 0)) for block in swapped]
        + [
            times,
            spec((None, rows, focal), lambda s: (0, s, 0)),
            spec((rows, 1), lambda s: (s, 0)),
        ],
        out_specs=[times, spec((focal, focal), lambda s: (0, 0))],
        scratch_shapes=[
            pltpu.VMEM((2 * chips, 2, rows, focal), jnp.float32),
            pltpu.VMEM((trace, rows, focal), jnp.float32),
            pltpu.VMEM((trace, rows, focal), jnp.bfloat16),
            pltpu.VMEM((focal, focal), jnp.float32),
        ],
        out_shape=[
            jax.ShapeDtypeStruct(initial.shape, jnp.bfloat16),
            jax.ShapeDtypeStruct((focal, focal), jnp.bfloat16),
        ],
        cost_estimate=pl.CostEstimate(
            flops=2 * trace * sub * focal * focal, bytes_accessed=4 << 20, transcendentals=0
        ),
        compiler_params=pltpu.CompilerParams(vmem_limit_bytes=14 << 20),
        name="series",
    )(*own, *swapped, initial, mutes, taper)


def second_kernel(*refs):
    for n, ref in enumerate(refs[:-1]):
        refs[-1][n] = ref[1]


def second_parts(blocks):
    shape = (len(blocks),) + blocks[0].shape[1:]
    return pl.pallas_call(
        second_kernel,
        in_specs=[spec()] * len(blocks),
        out_specs=spec(),
        out_shape=jax.ShapeDtypeStruct(shape, blocks[0].dtype),
        cost_estimate=pl.CostEstimate(flops=0, bytes_accessed=1 << 18, transcendentals=0),
        compiler_params=pltpu.CompilerParams(vmem_limit_bytes=2 << 20),
        name="second",
    )(*blocks)


def swap_cores(values, freq_count):
    return lax.ppermute(values, "freq", [(f, f ^ 1) for f in range(freq_count)])


def shift_chips(values, distance, freq_count):
    pairs = [(f, (f + 2 * distance) % freq_count) for f in range(freq_count)]
    return lax.ppermute(values, "freq", pairs)


def update(focal_field, v_factors, u_factors, ranks, tile_mask, initial_focus, mute_starts, taper):
    tile_count = lax.axis_size("tile")
    freq_count = lax.axis_size("freq")
    me = lax.axis_index("freq")
    chips = freq_count // 2
    place = jnp.stack([me // 2, lax.rem(me, 2)])
    _, _, focal_count = focal_field.shape[1:]
    u_rows = [flatten(place, u_factors[0], distances, chips) for distances in ORDER]
    coeffs = moments(ranks[0, :, 0], tile_mask[0, :, 0], focal_field[0], v_factors[0])
    received = lax.all_to_all(coeffs, "tile", split_axis=0, concat_axis=0, tiled=True)
    terms, u_rows[0] = rank_terms(received, u_rows[0], 1.0 / math.sqrt(freq_count))
    own, swapped = [None] * chips, []
    for n, distances in enumerate(ORDER):
        blocks = fields(terms, u_rows[n], distances)
        for d, block in zip(distances, blocks):
            own[d] = shift_chips(block, d, freq_count) if d else block
        swapped.append(swap_cores(second_parts([own[d] for d in distances]), freq_count))
    trace_length, group_rows = initial_focus.shape[1:3]
    normalizer = 1.0 / float(tile_count * trace_length * group_rows)
    focusing, partial = series_update(
        own, swapped, initial_focus, mute_starts, taper[0][:, None], normalizer
    )
    shares = lax.all_to_all(partial, "tile", split_axis=0, concat_axis=0, tiled=True)
    share_rows = focal_count // tile_count
    shares = shares.reshape(tile_count, 1, share_rows, focal_count)
    return (focusing, jnp.sum(shares.astype(jnp.float32), axis=0))


def solution(mesh):
    placed = (
        P("freq", "tile", None, None),
        P("freq", None, "tile", None),
        P("freq", "tile", None, None),
        P("freq", None, "tile"),
        P("freq", None, "tile"),
        P("tile", None, "freq", None),
        P("tile", "freq", None),
        P("tile", "freq"),
    )
    return jax.shard_map(
        update,
        mesh=mesh,
        in_specs=placed,
        out_specs=(P("tile", None, "freq", None), P("freq", "tile", None)),
        check_vma=False,
    )
```
